32 devices in a mesh: pole: 4 (over y, x), row: 8 (over z, core).
Axes of the slice: x: 2, y: 2, z: 4, core: 2. Of those that a mesh axis runs over, the one named last changes fastest.
Arguments:
- basis: bfloat16 [32768, 128], P('row'), may hold values from -24 to 24
- inverses: bfloat16 [4, 64, 512, 512], P('pole', 'row'), may hold values from -1.5 to 1.5
- lower: bfloat16 [64, 512, 512], P('row'), may hold values from -0.03955078 to 0.03955078
- upper: bfloat16 [64, 512, 512], P('row'), may hold values from -0.03955078 to 0.03955078
- pole_weights: float32 [4], P('pole'), may hold values from 0.5 to 1.5
Outputs:
- new_basis: float32 [32768, 128], P(('row', 'pole'))
The draws below stay inside these ranges and needn't reach their ends.
All inputs are finite; a program needn't handle non-finite values.
Results may differ from the reference program's by a relative error of at most 0.003.
Values may be sent and summed in bfloat16 or wider, within the bound.
A program may use at most 64 MiB of HBM per device.

```python
import math
import jax
import jax.numpy as jnp
from jax import lax

VECTORS = 128
BLOCK = 512
SWEEPS = 4
POLES = 4
NBLK = 64
NROWS = 32768


def draw_basis(key, part):
    first, second = jax.random.split(jax.random.fold_in(key, 11), 2)
    place = jnp.arange(NROWS, dtype=jnp.float32) / (NROWS - 1)
    factor = jnp.exp(jax.random.uniform(second, (NROWS,), jnp.float32, 0.0, math.log(4.0)))
    scales = (1.0 + 2.0 * place) * factor
    values = jnp.clip(jax.random.normal(first, (NROWS, VECTORS), jnp.float32), -6.0, 6.0)
    return (values * scales[:, None] / 3.0).astype(jnp.bfloat16)


def draw_inverses(key, part):
    first, second = jax.random.split(jax.random.fold_in(key, 23), 2)
    diag_values = jnp.exp(jax.random.uniform(first, (POLES, NBLK, BLOCK), jnp.float32, math.log(0.4), 0.0))
    spread = 0.15 / math.sqrt(BLOCK)
    rough = spread * jnp.clip(jax.random.normal(second, (POLES, NBLK, BLOCK, BLOCK), jnp.float32), -6.0, 6.0)
    eye = jnp.eye(BLOCK, dtype=jnp.float32)
    return (rough + eye * diag_values[..., None, :]).astype(jnp.bfloat16)


def steps_of(key, extent, cuts, smallest, largest):
    def one(dim, blocks):
        steps = jax.random.uniform(jax.random.fold_in(jax.random.fold_in(key, 6), dim), (blocks,), jnp.float32, smallest / len(cuts), largest / len(cuts))
        return jnp.repeat(jnp.exp(steps), extent[dim] // blocks).reshape((-1,) + (1,) * (len(extent) - dim - 1))

    level = one(*cuts[0])
    for cut in cuts[1:]:
        level = level * one(*cut)
    return level


def noise(rng, dims, scale, reach, shards=(), kind=jnp.bfloat16):
    values = jax.random.normal(rng, dims, jnp.float32) * scale
    if len(shards) > 0:
        values = steps_of(rng, dims, shards, -0.22, 0.18) * values
    return jnp.clip(values, min=-reach, max=reach).astype(kind)


def setup_inputs(seed: int = 0) -> dict:
    arg_keys = jax.random.split(jax.random.key(seed), 6)
    basis = draw_basis(jax.random.fold_in(arg_keys[5], 71), 0)
    inverses = draw_inverses(jax.random.fold_in(arg_keys[5], 71), 0)
    lower = noise(arg_keys[2], (NBLK, BLOCK, BLOCK), (0.3 / BLOCK ** 0.5), 0.03955078, ((0, 8),))
    upper = noise(arg_keys[3], (NBLK, BLOCK, BLOCK), (0.3 / BLOCK ** 0.5), 0.03955078, ((0, 8),))
    pole_weights = jnp.clip(0.5 + 1.0 * jax.random.uniform(arg_keys[4], (POLES,), jnp.float32) ** steps_of(arg_keys[4], (POLES,), ((0, 4),), -0.2, 0.2), 0.5, 1.5)
    return dict(basis=basis, inverses=inverses, lower=lower, upper=upper, pole_weights=pole_weights)


def reference(basis, inverses, lower, upper, pole_weights):
    blocks = basis.reshape(NBLK, BLOCK, VECTORS).astype(jnp.float32)
    lower_f = lower.astype(jnp.float32)
    upper_f = upper.astype(jnp.float32)

    def one_pole(total, item):
        inverse_f = item[0].astype(jnp.float32)
        state = jnp.einsum('bij,bjk->bik', inverse_f, blocks).astype(jnp.bfloat16)
        zero_block = jnp.zeros((1, BLOCK, VECTORS), jnp.bfloat16)
        for sweep in range(SWEEPS):
            before = jnp.concatenate([zero_block, state[:-1]], axis=0).astype(jnp.float32)
            after = jnp.concatenate([state[1:], zero_block], axis=0).astype(jnp.float32)
            rhs = blocks + jnp.einsum('bij,bjk->bik', lower_f, before) + jnp.einsum('bij,bjk->bik', upper_f, after)
            rhs = rhs.astype(jnp.bfloat16).astype(jnp.float32)
            state = jnp.einsum('bij,bjk->bik', inverse_f, rhs).astype(jnp.bfloat16)
        return (total + item[1] * state.astype(jnp.float32), None)
    start = jnp.zeros((NBLK, BLOCK, VECTORS), jnp.float32)
    total, unused = lax.scan(one_pole, start, (inverses, pole_weights))
    filtered = total.reshape(NROWS, VECTORS)
    gram = jnp.dot(filtered.T, filtered, precision=lax.Precision.HIGHEST) / NROWS
    factor = jnp.linalg.cholesky(gram)
    solved = jax.scipy.linalg.solve_triangular(factor, filtered.T, lower=True)
    return solved.T
```

```python
import functools

import jax
import jax.numpy as jnp
from jax import lax
from jax.experimental import pallas as pl
from jax.experimental.pallas import tpu as pltpu
from jax.sharding import PartitionSpec as P

SWEEPS = 4
MESH = pl.DeviceIdType.MESH
F32 = jnp.float32
BF16 = jnp.bfloat16
HIGHEST = lax.Precision.HIGHEST


def dot(a, b):
    return jnp.dot(a, b, preferred_element_type=F32)


def sweep_kernel(
    poles,
    rings,
    weight_ref,
    basis_hbm,
    inverse_hbm,
    lower_hbm,
    upper_hbm,
    mine_ref,
    gram_ref,
    basis,
    inverse,
    lower,
    upper,
    states,
    weights,
    got,
    partial,
    shares,
    piece,
    pieces,
    whole,
    load_sem,
    halo_send,
    halo_recv,
    weight_send,
    weight_recv,
    final_send,
    final_recv,
    share_send,
    share_recv,
    piece_send,
    piece_recv,
    whole_send,
    whole_recv,
):
    pole, row = lax.axis_index("pole"), lax.axis_index("row")
    count, size, width = basis.shape
    owned = count // poles
    pairs = count // 2
    has_left, has_right = row > 0, row < rings - 1

    def load(kind, b):
        source = (basis_hbm, inverse_hbm, lower_hbm, upper_hbm)[kind]
        target = (basis, inverse, lower, upper)[kind]
        return pltpu.make_async_copy(source.at[b], target.at[b], load_sem.at[kind, b])

    def send(src, dst, send_sem, recv_sem, **where):
        return pltpu.make_async_remote_copy(
            src_ref=src,
            dst_ref=dst,
            send_sem=send_sem,
            recv_sem=recv_sem,
            device_id=where,
            device_id_type=MESH,
        )

    for i in range(count):
        b = (i - 1) % count
        load(0, b).start()
        load(1, b).start()
    for i in range(count):
        b = (i + 1) % count
        load(2, b).start()
        load(3, b).start()

    weights[pole] = jnp.full(weights.shape[1:], weight_ref[0], F32)
    zero = jnp.zeros((size, width), BF16)

    @pl.when(jnp.logical_not(has_left))
    def _():
        for k in range(SWEEPS):
            states[k, 0] = zero

    @pl.when(jnp.logical_not(has_right))
    def _():
        for k in range(SWEEPS):
            states[k, count + 1] = zero

    barrier = pltpu.get_barrier_semaphore()
    for d in range(1, poles):
        pl.semaphore_signal(barrier, inc=1, device_id={"pole": lax.rem(pole + d, poles)}, device_id_type=MESH)
    for d in range(1, rings):
        pl.semaphore_signal(barrier, inc=1, device_id={"row": lax.rem(row + d, rings)}, device_id_type=MESH)

    def to_left(k):
        return send(
            states.at[k, 1], states.at[k, count + 1], halo_send.at[k, 0], halo_recv.at[k, 0], row=row - 1
        )

    def to_right(k):
        return send(states.at[k, count], states.at[k, 0], halo_send.at[k, 1], halo_recv.at[k, 1], row=row + 1)

    def send_halos(k):
        @pl.when(has_left)
        def _():
            to_left(k).start()

        @pl.when(has_right)
        def _():
            to_right(k).start()

    def first(i, carry):
        blocks = [lax.rem(2 * i + count - 1, count), lax.rem(2 * i, count)]
        for b in blocks:
            load(0, b).wait()
            load(1, b).wait()
        for b in blocks:
            states[0, b + 1] = dot(inverse[b], basis[b]).astype(BF16)

        @pl.when(i == 0)
        def _():
            pl.semaphore_wait(barrier, poles + rings - 2)
            send_halos(0)

        return carry

    lax.fori_loop(0, pairs, first, 0)

    for d in range(1, poles):
        send(
            weights.at[pole],
            weights.at[pole],
            weight_send.at[d],
            weight_recv.at[pole],
            pole=lax.rem(pole + d, poles),
        ).start()

    def final(b):
        return send(
            states.at[SWEEPS, b + 1],
            got.at[pole, lax.rem(b, owned)],
            final_send.at[b],
            final_recv.at[pole, lax.rem(b, owned)],
            pole=b // owned,
        )

    def sweep(t, carry):
        k = t // pairs + 1
        i = lax.rem(t, pairs)
        blocks = [lax.rem(2 * i + 1, count), lax.rem(2 * i + 2, count)]

        @pl.when(k == 1)
        def _():
            for b in blocks:
                load(2, b).wait()
                load(3, b).wait()

        @pl.when(jnp.logical_and(i == pairs - 1, has_left))
        def _():
            to_right(k - 1).wait_recv()

        @pl.when(jnp.logical_and(i == pairs - 1, has_right))
        def _():
            to_left(k - 1).wait_recv()

        for b in blocks:
            rhs = basis[b].astype(F32) + dot(lower[b], states[k - 1, b])
            rhs = rhs + dot(upper[b], states[k - 1, b + 2])
            states[k, b + 1] = dot(inverse[b], rhs.astype(BF16)).astype(BF16)

        @pl.when(jnp.logical_and(i == pairs - 1, k < SWEEPS))
        def _():
            send_halos(k)

        for b in blocks:

            @pl.when(jnp.logical_and(k == SWEEPS, b // owned != pole))
            def _():
                final(b).start()

        return carry

    lax.fori_loop(0, SWEEPS * pairs, sweep, 0)

    def weighted(p, block):
        return block.astype(F32) * weights[p, 0:1, :]

    others = [lax.rem(pole + d, poles) for d in range(1, poles)]
    for p in others:
        send(
            weights.at[p], weights.at[p], weight_send.at[0], weight_recv.at[p], pole=p
        ).wait_recv()
    total = jnp.zeros((width, width), F32)
    for j in range(owned):
        block = weighted(pole, states[SWEEPS, pole * owned + j + 1])
        for p in others:
            send(
                got.at[p, j], got.at[p, j], final_send.at[0], final_recv.at[p, j], pole=p
            ).wait_recv()
            block = block + weighted(p, got[p, j])
        mine_ref[j * size : (j + 1) * size, :] = block
        total = total + lax.dot_general(
            block, block, (((0,), (0,)), ((), ())), precision=HIGHEST, preferred_element_type=F32
        )

    lines = width // poles
    for q in range(poles):
        partial[q] = total[q * lines : (q + 1) * lines, :]

    def share_to(d):
        q = lax.rem(pole + d, poles)
        return send(partial.at[q], shares.at[pole], share_send.at[d], share_recv.at[pole], pole=q)

    for d in range(1, poles):
        share_to(d).start()
    part = partial[pole]
    for p in others:
        send(shares.at[p], shares.at[p], share_send.at[0], share_recv.at[p], pole=p).wait_recv()
        part = part + shares[p]
    piece[...] = part

    def piece_to(d):
        q = lax.rem(row + d, rings)
        return send(piece, pieces.at[row], piece_send.at[d], piece_recv.at[row], row=q)

    for d in range(1, rings):
        piece_to(d).start()
    for d in range(1, rings):
        p = lax.rem(row + d, rings)
        send(pieces.at[p], pieces.at[p], piece_send.at[0], piece_recv.at[p], row=p).wait_recv()
        part = part + pieces[p]
    whole[pole] = part

    def whole_to(d):
        q = lax.rem(pole + d, poles)
        return send(whole.at[pole], whole.at[pole], whole_send.at[d], whole_recv.at[pole], pole=q)

    for d in range(1, poles):
        whole_to(d).start()
    for p in others:
        send(whole.at[p], whole.at[p], whole_send.at[0], whole_recv.at[p], pole=p).wait_recv()
    scale = 1.0 / (count * size * rings)
    for q in range(poles):
        gram_ref[q * lines : (q + 1) * lines, :] = whole[q] * scale

    for k in range(SWEEPS):

        @pl.when(has_left)
        def _():
            to_left(k).wait_send()

        @pl.when(has_right)
        def _():
            to_right(k).wait_send()

    for b in range(count):

        @pl.when(b // owned != pole)
        def _():
            final(b).wait_send()

    for d in range(1, poles):
        send(
            weights.at[pole], weights.at[pole], weight_send.at[d], weight_recv.at[pole], pole=lax.rem(pole + d, poles)
        ).wait_send()
        share_to(d).wait_send()
        whole_to(d).wait_send()
    for d in range(1, rings):
        piece_to(d).wait_send()


def sweeps_and_gram(basis, inverse, lower, upper, pole_weights):
    poles, rings = lax.axis_size("pole"), lax.axis_size("row")
    count, size, width = basis.shape
    owned = count // poles
    lines = width // poles
    dma = pltpu.SemaphoreType.DMA
    anywhere = pl.BlockSpec(memory_space=pl.ANY)
    return pl.pallas_call(
        functools.partial(sweep_kernel, poles, rings),
        out_shape=(
            jax.ShapeDtypeStruct((owned * size, width), F32),
            jax.ShapeDtypeStruct((width, width), F32),
        ),
        in_specs=[pl.BlockSpec(memory_space=pltpu.SMEM)] + [anywhere] * 4,
        out_specs=(pl.BlockSpec(memory_space=pltpu.VMEM),) * 2,
        scratch_shapes=[
            pltpu.VMEM((count, size, width), BF16),
            pltpu.VMEM((count, size, size), BF16),
            pltpu.VMEM((count, size, size), BF16),
            pltpu.VMEM((count, size, size), BF16),
            pltpu.VMEM((SWEEPS + 1, count + 2, size, width), BF16),
            pltpu.VMEM((poles, 8, width), F32),
            pltpu.VMEM((poles, owned, size, width), BF16),
            pltpu.VMEM((poles, lines, width), F32),
            pltpu.VMEM((poles, lines, width), F32),
            pltpu.VMEM((lines, width), F32),
            pltpu.VMEM((rings, lines, width), F32),
            pltpu.VMEM((poles, lines, width), F32),
            dma((4, count)),
            dma((SWEEPS, 2)),
            dma((SWEEPS, 2)),
            dma((poles,)),
            dma((poles,)),
            dma((count,)),
            dma((poles, owned)),
            dma((poles,)),
            dma((poles,)),
            dma((rings,)),
            dma((rings,)),
            dma((poles,)),
            dma((poles,)),
        ],
        compiler_params=pltpu.CompilerParams(collective_id=0, has_side_effects=True),
        name="sweeps",
    )(pole_weights, basis, inverse, lower, upper)


def shards(basis, inverses, lower, upper, pole_weights):
    rows, width = basis.shape
    count, size = inverses.shape[1], inverses.shape[-1]
    mine, gram = sweeps_and_gram(
        basis.reshape(count, size, width), inverses[0], lower, upper, pole_weights
    )
    factor = jnp.linalg.cholesky(gram)
    solved = jax.scipy.linalg.solve_triangular(factor, mine.T, lower=True)
    return solved.T


def solution(mesh):
    return jax.shard_map(
        shards,
        mesh=mesh,
        in_specs=(
            P("row", None),
            P("pole", "row", None, None),
            P("row", None, None),
            P("row", None, None),
            P("pole"),
        ),
        out_specs=P(("row", "pole"), None),
        check_vma=False,
    )
```

```python
import functools

import jax
import jax.numpy as jnp
from jax import lax
from jax.experimental import pallas as pl
from jax.experimental.pallas import tpu as pltpu
from jax.sharding import PartitionSpec as P

SWEEPS = 4
MESH = pl.DeviceIdType.MESH
F32 = jnp.float32
BF16 = jnp.bfloat16
HIGHEST = lax.Precision.HIGHEST


def dot(a, b):
    return jnp.dot(a, b, preferred_element_type=F32)


def sweep_kernel(
    poles,
    rings,
    weight_ref,
    basis_hbm,
    inverse_hbm,
    lower_hbm,
    upper_hbm,
    mine_ref,
    gram_ref,
    basis,
    inverse,
    lower,
    upper,
    states,
    weights,
    got,
    partial,
    shares,
    piece,
    pieces,
    whole,
    load_sem,
    halo_send,
    halo_recv,
    weight_send,
    weight_recv,
    final_send,
    final_recv,
    share_send,
    share_recv,
    piece_send,
    piece_recv,
    whole_send,
    whole_recv,
):
    pole, row = lax.axis_index("pole"), lax.axis_index("row")
    count, size, width = basis.shape
    owned = count // poles
    pairs = count // 2
    has_left, has_right = row > 0, row < rings - 1

    def load(kind, b):
        source = (basis_hbm, inverse_hbm, lower_hbm, upper_hbm)[kind]
        target = (basis, inverse, lower, upper)[kind]
        return pltpu.make_async_copy(source.at[b], target.at[b], load_sem.at[kind, b])

    def send(src, dst, send_sem, recv_sem, **where):
        return pltpu.make_async_remote_copy(
            src_ref=src,
            dst_ref=dst,
            send_sem=send_sem,
            recv_sem=recv_sem,
            device_id=where,
            device_id_type=MESH,
        )

    for i in range(count):
        b = (i - 1) % count
        load(0, b).start()
        load(1, b).start()
    for i in range(count):
        b = (i + 1) % count
        load(2, b).start()
        load(3, b).start()

    weights[pole] = jnp.full(weights.shape[1:], weight_ref[0], F32)
    zero = jnp.zeros((size, width), BF16)

    @pl.when(jnp.logical_not(has_left))
    def _():
        for k in range(SWEEPS):
            states[k, 0] = zero

    @pl.when(jnp.logical_not(has_right))
    def _():
        for k in range(SWEEPS):
            states[k, count + 1] = zero

    barrier = pltpu.get_barrier_semaphore()
    for d in range(1, poles):
        pl.semaphore_signal(barrier, inc=1, device_id={"pole": lax.rem(pole + d, poles)}, device_id_type=MESH)
    for d in range(1, rings):
        pl.semaphore_signal(barrier, inc=1, device_id={"row": lax.rem(row + d, rings)}, device_id_type=MESH)

    def to_left(k):
        return send(
            states.at[k, 1], states.at[k, count + 1], halo_send.at[k, 0], halo_recv.at[k, 0], row=row - 1
        )

    def to_right(k):
        return send(states.at[k, count], states.at[k, 0], halo_send.at[k, 1], halo_recv.at[k, 1], row=row + 1)

    def send_halos(k):
        @pl.when(has_left)
        def _():
            to_left(k).start()

        @pl.when(has_right)
        def _():
            to_right(k).start()

    def first(i, carry):
        blocks = [lax.rem(2 * i + count - 1, count), lax.rem(2 * i, count)]
        for b in blocks:
            load(0, b).wait()
            load(1, b).wait()
        for b in blocks:
            states[0, b + 1] = dot(inverse[b], basis[b]).astype(BF16)

        @pl.when(i == 0)
        def _():
            pl.semaphore_wait(barrier, poles + rings - 2)
            send_halos(0)

        return carry

    lax.fori_loop(0, pairs, first, 0)

    for d in range(1, poles):
        send(
            weights.at[pole],
            weights.at[pole],
            weight_send.at[d],
            weight_recv.at[pole],
            pole=lax.rem(pole + d, poles),
        ).start()

    def final(b):
        return send(
            states.at[SWEEPS, b + 1],
            got.at[pole, lax.rem(b, owned)],
            final_send.at[b],
            final_recv.at[pole, lax.rem(b, owned)],
            pole=b // owned,
        )

    def sweep(t, carry):
        k = t // pairs + 1
        i = lax.rem(t, pairs)
        blocks = [lax.rem(2 * i + 1, count), lax.rem(2 * i + 2, count)]

        @pl.when(k == 1)
        def _():
            for b in blocks:
                load(2, b).wait()
                load(3, b).wait()

        @pl.when(jnp.logical_and(i == pairs - 1, has_left))
        def _():
            to_right(k - 1).wait_recv()

        @pl.when(jnp.logical_and(i == pairs - 1, has_right))
        def _():
            to_left(k - 1).wait_recv()

        for b in blocks:
            rhs = basis[b].astype(F32) + dot(lower[b], states[k - 1, b])
            rhs = rhs + dot(upper[b], states[k - 1, b + 2])
            states[k, b + 1] = dot(inverse[b], rhs.astype(BF16)).astype(BF16)

        @pl.when(jnp.logical_and(i == pairs - 1, k < SWEEPS))
        def _():
            send_halos(k)

        for b in blocks:

            @pl.when(jnp.logical_and(k == SWEEPS, b // owned != pole))
            def _():
                final(b).start()

        return carry

    lax.fori_loop(0, SWEEPS * pairs, sweep, 0)

    def weighted(p, block):
        return block.astype(F32) * weights[p, 0:1, :]

    others = [lax.rem(pole + d, poles) for d in range(1, poles)]
    for p in others:
        send(
            weights.at[p], weights.at[p], weight_send.at[0], weight_recv.at[p], pole=p
        ).wait_recv()
    total = jnp.zeros((width, width), F32)
    for j in range(owned):
        block = weighted(pole, states[SWEEPS, pole * owned + j + 1])
        for p in others:
            send(
                got.at[p, j], got.at[p, j], final_send.at[0], final_recv.at[p, j], pole=p
            ).wait_recv()
            block = block + weighted(p, got[p, j])
        mine_ref[j * size : (j + 1) * size, :] = block
        total = total + lax.dot_general(
            block, block, (((0,), (0,)), ((), ())), precision=HIGHEST, preferred_element_type=F32
        )

    lines = width // poles
    for q in range(poles):
        partial[q] = total[q * lines : (q + 1) * lines, :]

    def share_to(d):
        q = lax.rem(pole + d, poles)
        return send(partial.at[q], shares.at[pole], share_send.at[d], share_recv.at[pole], pole=q)

    for d in range(1, poles):
        share_to(d).start()
    part = partial[pole]
    for p in others:
        send(shares.at[p], shares.at[p], share_send.at[0], share_recv.at[p], pole=p).wait_recv()
        part = part + shares[p]
    piece[...] = part

    def piece_to(d):
        q = lax.rem(row + d, rings)
        return send(piece, pieces.at[row], piece_send.at[d], piece_recv.at[row], row=q)

    for d in range(1, rings):
        piece_to(d).start()
    for d in range(1, rings):
        p = lax.rem(row + d, rings)
        send(pieces.at[p], pieces.at[p], piece_send.at[0], piece_recv.at[p], row=p).wait_recv()
        part = part + pieces[p]
    whole[pole] = part

    def whole_to(d):
        q = lax.rem(pole + d, poles)
        return send(whole.at[pole], whole.at[pole], whole_send.at[d], whole_recv.at[pole], pole=q)

    for d in range(1, poles):
        whole_to(d).start()
    for p in others:
        send(whole.at[p], whole.at[p], whole_send.at[0], whole_recv.at[p], pole=p).wait_recv()
    scale = 1.0 / (count * size * rings)
    for q in range(poles):
        gram_ref[q * lines : (q + 1) * lines, :] = whole[q] * scale

    for k in range(SWEEPS):

        @pl.when(has_left)
        def _():
            to_left(k).wait_send()

        @pl.when(has_right)
        def _():
            to_right(k).wait_send()

    for b in range(count):

        @pl.when(b // owned != pole)
        def _():
            final(b).wait_send()

    for d in range(1, poles):
        send(
            weights.at[pole], weights.at[pole], weight_send.at[d], weight_recv.at[pole], pole=lax.rem(pole + d, poles)
        ).wait_send()
        share_to(d).wait_send()
        whole_to(d).wait_send()
    for d in range(1, rings):
        piece_to(d).wait_send()


def sweeps_and_gram(basis, inverse, lower, upper, pole_weights):
    poles, rings = lax.axis_size("pole"), lax.axis_size("row")
    count, size, width = basis.shape
    owned = count // poles
    lines = width // poles
    dma = pltpu.SemaphoreType.DMA
    anywhere = pl.BlockSpec(memory_space=pl.ANY)
    return pl.pallas_call(
        functools.partial(sweep_kernel, poles, rings),
        out_shape=(
            jax.ShapeDtypeStruct((owned * size, width), F32),
            jax.ShapeDtypeStruct((width, width), F32),
        ),
        in_specs=[pl.BlockSpec(memory_space=pltpu.SMEM)] + [anywhere] * 4,
        out_specs=(pl.BlockSpec(memory_space=pltpu.VMEM),) * 2,
        scratch_shapes=[
            pltpu.VMEM((count, size, width), BF16),
            pltpu.VMEM((count, size, size), BF16),
            pltpu.VMEM((count, size, size), BF16),
            pltpu.VMEM((count, size, size), BF16),
            pltpu.VMEM((SWEEPS + 1, count + 2, size, width), BF16),
            pltpu.VMEM((poles, 8, width), F32),
            pltpu.VMEM((poles, owned, size, width), BF16),
            pltpu.VMEM((poles, lines, width), F32),
            pltpu.VMEM((poles, lines, width), F32),
            pltpu.VMEM((lines, width), F32),
            pltpu.VMEM((rings, lines, width), F32),
            pltpu.VMEM((poles, lines, width), F32),
            dma((4, count)),
            dma((SWEEPS, 2)),
            dma((SWEEPS, 2)),
            dma((poles,)),
            dma((poles,)),
            dma((count,)),
            dma((poles, owned)),
            dma((poles,)),
            dma((poles,)),
            dma((rings,)),
            dma((rings,)),
            dma((poles,)),
            dma((poles,)),
        ],
        compiler_params=pltpu.CompilerParams(collective_id=0, has_side_effects=True),
        name="sweeps",
    )(pole_weights, basis, inverse, lower, upper)


def inverse_factor(gram):
    n = gram.shape[0]
    lane = lax.broadcasted_iota(jnp.int32, (8, n), 1)
    sub = lax.broadcasted_iota(jnp.int32, (8, n), 0)
    lane1 = lane[0:1]
    rows = [gram[g:g+8] for g in range(0, n, 8)]
    for g in range(n // 8):
        base = 8 * g
        t = rows[g]
        cols = [jnp.broadcast_to(t[:, base+k:base+k+1], (8, n)) for k in range(8)]
        ratios, tops = {}, []
        for k in range(8):
            inv = 1.0 / cols[k][k:k+1]
            top = jnp.where(lane1 == base + k, inv, t[k:k+1] * inv)
            below = jnp.where(sub > k, cols[k], 0.0)
            t = jnp.where((lane == base + k) & (sub > k), 0.0, t) - below * top
            for l in range(k+1, 8):
                ratios[k, l] = cols[l][k:k+1] * inv
                cols[l] = cols[l] - below * ratios[k, l]
            tops.append(jnp.where((lane1 > base + k) & (lane1 < base + 8), 0.0, top))
        rows[g] = t
        inside = (lane >= base) & (lane < base + 8)
        for h in range(g+1, n // 8):
            t = rows[h]
            c = [jnp.broadcast_to(t[:, base+k:base+k+1], (8, n)) for k in range(8)]
            t = jnp.where(inside, 0.0, t)
            for k in range(8):
                t = t - c[k] * tops[k]
                for l in range(k+1, 8):
                    c[l] = c[l] - c[k] * ratios[k, l]
            rows[h] = t
    out = []
    for g, t in enumerate(rows):
        row = sub + 8 * g
        root = lax.rsqrt(jnp.sum(jnp.where(lane == row, t, 0.0), axis=1, keepdims=True))
        out.append(jnp.where(lane < row, t, jnp.where(lane == row, 1.0, 0.0)) * root)
    return jnp.concatenate(out, axis=0)


def solve_kernel(mine_ref, gram_ref, out_ref):
    inverse = inverse_factor(gram_ref[...])
    out_ref[...] = lax.dot_general(
        mine_ref[...], inverse, (((1,), (1,)), ((), ())), precision=HIGHEST, preferred_element_type=F32
    )


def orthonormalize(mine, gram):
    vmem = pl.BlockSpec(memory_space=pltpu.VMEM)
    return pl.pallas_call(
        solve_kernel,
        out_shape=jax.ShapeDtypeStruct(mine.shape, F32),
        in_specs=[vmem] * 2,
        out_specs=vmem,
        name="orthonormalize",
    )(mine, gram)


def shards(basis, inverses, lower, upper, pole_weights):
    rows, width = basis.shape
    count, size = inverses.shape[1], inverses.shape[-1]
    mine, gram = sweeps_and_gram(
        basis.reshape(count, size, width), inverses[0], lower, upper, pole_weights
    )
    return orthonormalize(mine, gram)


def solution(mesh):
    return jax.shard_map(
        shards,
        mesh=mesh,
        in_specs=(
            P("row", None),
            P("pole", "row", None, None),
            P("row", None, None),
            P("row", None, None),
            P("pole"),
        ),
        out_specs=P(("row", "pole"), None),
        check_vma=False,
    )
```

```python
import functools

import jax
import jax.numpy as jnp
from jax import lax
from jax.experimental import pallas as pl
from jax.experimental.pallas import tpu as pltpu
from jax.sharding import PartitionSpec as P

SWEEPS = 4
MESH = pl.DeviceIdType.MESH
F32 = jnp.float32
BF16 = jnp.bfloat16
HIGHEST = lax.Precision.HIGHEST


def dot(a, b):
    return jnp.dot(a, b, preferred_element_type=F32)


def sweep_kernel(
    poles,
    rings,
    weight_ref,
    basis_hbm,
    inverse_hbm,
    lower_hbm,
    upper_hbm,
    mine_ref,
    gram_ref,
    basis,
    inverse,
    lower,
    upper,
    states,
    weights,
    got,
    partial,
    shares,
    piece,
    pieces,
    whole,
    load_sem,
    halo_send,
    halo_recv,
    weight_send,
    weight_recv,
    final_send,
    final_recv,
    share_send,
    share_recv,
    piece_send,
    piece_recv,
    whole_send,
    whole_recv,
):
    pole, row = lax.axis_index("pole"), lax.axis_index("row")
    count, size, width = basis.shape
    owned = count // poles
    has_left, has_right = row > 0, row < rings - 1

    def load(kind, b):
        source = (basis_hbm, inverse_hbm, lower_hbm, upper_hbm)[kind]
        target = (basis, inverse, lower, upper)[kind]
        return pltpu.make_async_copy(source.at[b], target.at[b], load_sem.at[kind, b])

    def send(src, dst, send_sem, recv_sem, **where):
        return pltpu.make_async_remote_copy(
            src_ref=src,
            dst_ref=dst,
            send_sem=send_sem,
            recv_sem=recv_sem,
            device_id=where,
            device_id_type=MESH,
        )

    for i in range(count):
        b = (i - 1) % count
        load(0, b).start()
        load(1, b).start()
    for i in range(count):
        b = (i + 1) % count
        load(2, b).start()
        load(3, b).start()

    weights[pole] = jnp.full(weights.shape[1:], weight_ref[0], F32)
    zero = jnp.zeros((size, width), BF16)

    @pl.when(jnp.logical_not(has_left))
    def _():
        for k in range(SWEEPS):
            states[k, 0] = zero

    @pl.when(jnp.logical_not(has_right))
    def _():
        for k in range(SWEEPS):
            states[k, count + 1] = zero

    barrier = pltpu.get_barrier_semaphore()
    for d in range(1, poles):
        pl.semaphore_signal(barrier, inc=1, device_id={"pole": lax.rem(pole + d, poles)}, device_id_type=MESH)
    for d in range(1, rings):
        pl.semaphore_signal(barrier, inc=1, device_id={"row": lax.rem(row + d, rings)}, device_id_type=MESH)

    def to_left(k):
        return send(
            states.at[k, 1], states.at[k, count + 1], halo_send.at[k, 0], halo_recv.at[k, 0], row=row - 1
        )

    def to_right(k):
        return send(states.at[k, count], states.at[k, 0], halo_send.at[k, 1], halo_recv.at[k, 1], row=row + 1)

    def send_halos(k):
        @pl.when(has_left)
        def _():
            to_left(k).start()

        @pl.when(has_right)
        def _():
            to_right(k).start()

    edge = sorted({0, count - 1})
    inner = list(range(1, count - 1))
    for blocks in [edge] + [inner[j : j + 3] for j in range(0, len(inner), 3)]:
        for b in blocks:
            load(0, b).wait()
            load(1, b).wait()
        starts = [dot(inverse[b], basis[b]).astype(BF16) for b in blocks]
        for b, start in zip(blocks, starts):
            states[0, b + 1] = start
        if blocks is edge:
            pl.semaphore_wait(barrier, poles + rings - 2)
            send_halos(0)

    for d in range(1, poles):
        send(
            weights.at[pole],
            weights.at[pole],
            weight_send.at[d],
            weight_recv.at[pole],
            pole=lax.rem(pole + d, poles),
        ).start()

    def final(b):
        return send(
            states.at[SWEEPS, b + 1],
            got.at[pole, b % owned],
            final_send.at[b],
            final_recv.at[pole, b % owned],
            pole=b // owned,
        )

    def below(k, b):
        return dot(lower[b], states[k - 1, b])

    def above(k, b):
        return dot(upper[b], states[k - 1, b + 2])

    def send_finals(blocks):
        for b in blocks:

            @pl.when(b // owned != pole)
            def _():
                final(b).start()

    def sweep(k, groups, loading=False, last=False):
        for blocks in groups:
            if loading:
                for b in blocks:
                    load(2, b).wait()
                    load(3, b).wait()
            sides = [(basis[b].astype(F32) + below(k, b) + above(k, b)).astype(BF16) for b in blocks]
            if blocks is groups[-1]:
                if loading:
                    for b in edge:
                        load(2, b).wait()
                        load(3, b).wait()
                head = basis[0].astype(F32) + above(k, 0)
                tail = basis[count - 1].astype(F32) + below(k, count - 1)
            fresh = [dot(inverse[b], side).astype(BF16) for b, side in zip(blocks, sides)]
            for b, value in zip(blocks, fresh):
                states[k, b + 1] = value
            if last:
                send_finals(blocks)

        @pl.when(has_left)
        def _():
            to_right(k - 1).wait_recv()

        @pl.when(has_right)
        def _():
            to_left(k - 1).wait_recv()

        head = (head + below(k, 0)).astype(BF16)
        tail = (tail + above(k, count - 1)).astype(BF16)
        head = dot(inverse[0], head).astype(BF16)
        tail = dot(inverse[count - 1], tail).astype(BF16)
        states[k, 1] = head
        states[k, count] = tail
        if last:
            send_finals(edge)
        else:
            send_halos(k)

    halves = [inner[: len(inner) // 2], inner[len(inner) // 2 :]]
    sweep(1, halves, loading=True)

    def middle(k, carry):
        sweep(k, [inner])
        return carry

    lax.fori_loop(2, SWEEPS, middle, 0)
    sweep(SWEEPS, halves, last=True)

    def weighted(p, block):
        return block.astype(F32) * weights[p, 0:1, :]

    others = [lax.rem(pole + d, poles) for d in range(1, poles)]
    for p in others:
        send(
            weights.at[p], weights.at[p], weight_send.at[0], weight_recv.at[p], pole=p
        ).wait_recv()
    total = jnp.zeros((width, width), F32)
    for j in range(owned):
        block = weighted(pole, states[SWEEPS, pole * owned + j + 1])
        for p in others:
            send(
                got.at[p, j], got.at[p, j], final_send.at[0], final_recv.at[p, j], pole=p
            ).wait_recv()
            block = block + weighted(p, got[p, j])
        mine_ref[j * size : (j + 1) * size, :] = block
        total = total + lax.dot_general(
            block, block, (((0,), (0,)), ((), ())), precision=HIGHEST, preferred_element_type=F32
        )

    lines = width // poles
    for q in range(poles):
        partial[q] = total[q * lines : (q + 1) * lines, :]

    def share_to(d):
        q = lax.rem(pole + d, poles)
        return send(partial.at[q], shares.at[pole], share_send.at[d], share_recv.at[pole], pole=q)

    for d in range(1, poles):
        share_to(d).start()
    part = partial[pole]
    for p in others:
        send(shares.at[p], shares.at[p], share_send.at[0], share_recv.at[p], pole=p).wait_recv()
        part = part + shares[p]
    piece[...] = part

    def piece_to(d):
        q = lax.rem(row + d, rings)
        return send(piece, pieces.at[row], piece_send.at[d], piece_recv.at[row], row=q)

    for d in range(1, rings):
        piece_to(d).start()
    for d in range(1, rings):
        p = lax.rem(row + d, rings)
        send(pieces.at[p], pieces.at[p], piece_send.at[0], piece_recv.at[p], row=p).wait_recv()
        part = part + pieces[p]
    whole[pole] = part

    def whole_to(d):
        q = lax.rem(pole + d, poles)
        return send(whole.at[pole], whole.at[pole], whole_send.at[d], whole_recv.at[pole], pole=q)

    for d in range(1, poles):
        whole_to(d).start()
    for p in others:
        send(whole.at[p], whole.at[p], whole_send.at[0], whole_recv.at[p], pole=p).wait_recv()
    scale = 1.0 / (count * size * rings)
    for q in range(poles):
        gram_ref[q * lines : (q + 1) * lines, :] = whole[q] * scale

    for k in range(SWEEPS):

        @pl.when(has_left)
        def _():
            to_left(k).wait_send()

        @pl.when(has_right)
        def _():
            to_right(k).wait_send()

    for b in range(count):

        @pl.when(b // owned != pole)
        def _():
            final(b).wait_send()

    for d in range(1, poles):
        send(
            weights.at[pole], weights.at[pole], weight_send.at[d], weight_recv.at[pole], pole=lax.rem(pole + d, poles)
        ).wait_send()
        share_to(d).wait_send()
        whole_to(d).wait_send()
    for d in range(1, rings):
        piece_to(d).wait_send()


def sweeps_and_gram(basis, inverse, lower, upper, pole_weights):
    poles, rings = lax.axis_size("pole"), lax.axis_size("row")
    count, size, width = basis.shape
    owned = count // poles
    lines = width // poles
    dma = pltpu.SemaphoreType.DMA
    anywhere = pl.BlockSpec(memory_space=pl.ANY)
    return pl.pallas_call(
        functools.partial(sweep_kernel, poles, rings),
        out_shape=(
            jax.ShapeDtypeStruct((owned * size, width), F32),
            jax.ShapeDtypeStruct((width, width), F32),
        ),
        in_specs=[pl.BlockSpec(memory_space=pltpu.SMEM)] + [anywhere] * 4,
        out_specs=(pl.BlockSpec(memory_space=pltpu.VMEM),) * 2,
        scratch_shapes=[
            pltpu.VMEM((count, size, width), BF16),
            pltpu.VMEM((count, size, size), BF16),
            pltpu.VMEM((count, size, size), BF16),
            pltpu.VMEM((count, size, size), BF16),
            pltpu.VMEM((SWEEPS + 1, count + 2, size, width), BF16),
            pltpu.VMEM((poles, 8, width), F32),
            pltpu.VMEM((poles, owned, size, width), BF16),
            pltpu.VMEM((poles, lines, width), F32),
            pltpu.VMEM((poles, lines, width), F32),
            pltpu.VMEM((lines, width), F32),
            pltpu.VMEM((rings, lines, width), F32),
            pltpu.VMEM((poles, lines, width), F32),
            dma((4, count)),
            dma((SWEEPS, 2)),
            dma((SWEEPS, 2)),
            dma((poles,)),
            dma((poles,)),
            dma((count,)),
            dma((poles, owned)),
            dma((poles,)),
            dma((poles,)),
            dma((rings,)),
            dma((rings,)),
            dma((poles,)),
            dma((poles,)),
        ],
        compiler_params=pltpu.CompilerParams(collective_id=0, has_side_effects=True),
        name="sweeps",
    )(pole_weights, basis, inverse, lower, upper)


def inverse_factor(gram):
    n = gram.shape[0]
    lane = lax.broadcasted_iota(jnp.int32, (8, n), 1)
    sub = lax.broadcasted_iota(jnp.int32, (8, n), 0)
    lane1 = lane[0:1]
    rows = [gram[g:g+8] for g in range(0, n, 8)]
    for g in range(n // 8):
        base = 8 * g
        t = rows[g]
        cols = [jnp.broadcast_to(t[:, base+k:base+k+1], (8, n)) for k in range(8)]
        ratios, tops = {}, []
        for k in range(8):
            inv = 1.0 / cols[k][k:k+1]
            top = jnp.where(lane1 == base + k, inv, t[k:k+1] * inv)
            below = jnp.where(sub > k, cols[k], 0.0)
            t = jnp.where((lane == base + k) & (sub > k), 0.0, t) - below * top
            for l in range(k+1, 8):
                ratios[k, l] = cols[l][k:k+1] * inv
                cols[l] = cols[l] - below * ratios[k, l]
            tops.append(jnp.where((lane1 > base + k) & (lane1 < base + 8), 0.0, top))
        rows[g] = t
        inside = (lane >= base) & (lane < base + 8)
        for h in range(g+1, n // 8):
            t = rows[h]
            c = [jnp.broadcast_to(t[:, base+k:base+k+1], (8, n)) for k in range(8)]
            t = jnp.where(inside, 0.0, t)
            for k in range(8):
                t = t - c[k] * tops[k]
                for l in range(k+1, 8):
                    c[l] = c[l] - c[k] * ratios[k, l]
            rows[h] = t
    out = []
    for g, t in enumerate(rows):
        row = sub + 8 * g
        root = lax.rsqrt(jnp.sum(jnp.where(lane == row, t, 0.0), axis=1, keepdims=True))
        out.append(jnp.where(lane < row, t, jnp.where(lane == row, 1.0, 0.0)) * root)
    return jnp.concatenate(out, axis=0)


def solve_kernel(mine_ref, gram_ref, out_ref):
    inverse = inverse_factor(gram_ref[...])
    out_ref[...] = lax.dot_general(
        mine_ref[...], inverse, (((1,), (1,)), ((), ())), precision=HIGHEST, preferred_element_type=F32
    )


def orthonormalize(mine, gram):
    vmem = pl.BlockSpec(memory_space=pltpu.VMEM)
    return pl.pallas_call(
        solve_kernel,
        out_shape=jax.ShapeDtypeStruct(mine.shape, F32),
        in_specs=[vmem] * 2,
        out_specs=vmem,
        name="orthonormalize",
    )(mine, gram)


def shards(basis, inverses, lower, upper, pole_weights):
    rows, width = basis.shape
    count, size = inverses.shape[1], inverses.shape[-1]
    mine, gram = sweeps_and_gram(
        basis.reshape(count, size, width), inverses[0], lower, upper, pole_weights
    )
    return orthonormalize(mine, gram)


def solution(mesh):
    return jax.shard_map(
        shards,
        mesh=mesh,
        in_specs=(
            P("row", None),
            P("pole", "row", None, None),
            P("row", None, None),
            P("row", None, None),
            P("pole"),
        ),
        out_specs=P(("row", "pole"), None),
        check_vma=False,
    )
```

```python
import functools

import jax
import jax.numpy as jnp
from jax import lax
from jax.experimental import pallas as pl
from jax.experimental.pallas import tpu as pltpu
from jax.sharding import PartitionSpec as P

SWEEPS = 4
MESH = pl.DeviceIdType.MESH
F32 = jnp.float32
BF16 = jnp.bfloat16
HIGHEST = lax.Precision.HIGHEST


def dot(a, b):
    return jnp.dot(a, b, preferred_element_type=F32)


def sweep_kernel(
    poles,
    rings,
    weight_ref,
    basis_hbm,
    inverse_hbm,
    lower_hbm,
    upper_hbm,
    mine_ref,
    gram_ref,
    basis,
    inverse,
    lower,
    upper,
    states,
    weights,
    got,
    partial,
    shares,
    piece,
    pieces,
    whole,
    load_sem,
    halo_send,
    halo_recv,
    weight_send,
    weight_recv,
    final_send,
    final_recv,
    share_send,
    share_recv,
    piece_send,
    piece_recv,
    whole_send,
    whole_recv,
):
    pole, row = lax.axis_index("pole"), lax.axis_index("row")
    count, size, width = basis.shape
    owned = count // poles
    has_left, has_right = row > 0, row < rings - 1

    def load(kind, b):
        source = (basis_hbm, inverse_hbm, lower_hbm, upper_hbm)[kind]
        target = (basis, inverse, lower, upper)[kind]
        return pltpu.make_async_copy(source.at[b], target.at[b], load_sem.at[kind, b])

    def send(src, dst, send_sem, recv_sem, **where):
        return pltpu.make_async_remote_copy(
            src_ref=src,
            dst_ref=dst,
            send_sem=send_sem,
            recv_sem=recv_sem,
            device_id=where,
            device_id_type=MESH,
        )

    for i in range(count):
        b = (i - 1) % count
        load(0, b).start()
        load(1, b).start()
    for i in range(count):
        b = (i + 1) % count
        load(2, b).start()
        load(3, b).start()

    weights[pole] = jnp.full(weights.shape[1:], weight_ref[0], F32)
    zero = jnp.zeros((size, width), BF16)

    @pl.when(jnp.logical_not(has_left))
    def _():
        for k in range(SWEEPS):
            states[k, 0] = zero

    @pl.when(jnp.logical_not(has_right))
    def _():
        for k in range(SWEEPS):
            states[k, count + 1] = zero

    barrier = pltpu.get_barrier_semaphore()
    for d in range(1, poles):
        pl.semaphore_signal(barrier, inc=1, device_id={"pole": lax.rem(pole + d, poles)}, device_id_type=MESH)
    for d in range(1, rings):
        pl.semaphore_signal(barrier, inc=1, device_id={"row": lax.rem(row + d, rings)}, device_id_type=MESH)

    def to_left(k):
        return send(
            states.at[k, 1], states.at[k, count + 1], halo_send.at[k, 0], halo_recv.at[k, 0], row=row - 1
        )

    def to_right(k):
        return send(states.at[k, count], states.at[k, 0], halo_send.at[k, 1], halo_recv.at[k, 1], row=row + 1)

    def send_halos(k):
        @pl.when(has_left)
        def _():
            to_left(k).start()

        @pl.when(has_right)
        def _():
            to_right(k).start()

    edge = sorted({0, count - 1})
    inner = list(range(1, count - 1))
    for blocks in [edge] + [inner[j : j + 3] for j in range(0, len(inner), 3)]:
        for b in blocks:
            load(0, b).wait()
            load(1, b).wait()
        starts = [dot(inverse[b], basis[b]).astype(BF16) for b in blocks]
        for b, start in zip(blocks, starts):
            states[0, b + 1] = start
        if blocks is edge:
            pl.semaphore_wait(barrier, poles + rings - 2)
            send_halos(0)

    for d in range(1, poles):
        send(
            weights.at[pole],
            weights.at[pole],
            weight_send.at[d],
            weight_recv.at[pole],
            pole=lax.rem(pole + d, poles),
        ).start()

    def final(b):
        return send(
            states.at[SWEEPS, b + 1],
            got.at[pole, b % owned],
            final_send.at[b],
            final_recv.at[pole, b % owned],
            pole=b // owned,
        )

    def below(k, b):
        return dot(lower[b], states[k - 1, b])

    def above(k, b):
        return dot(upper[b], states[k - 1, b + 2])

    def send_finals(blocks):
        for b in blocks:

            @pl.when(b // owned != pole)
            def _():
                final(b).start()

    def sweep(k, groups, loading=False, last=False, between=None):
        for blocks in groups:
            if loading:
                for b in blocks:
                    load(2, b).wait()
                    load(3, b).wait()
            sides = [(basis[b].astype(F32) + below(k, b) + above(k, b)).astype(BF16) for b in blocks]
            if blocks is groups[-1]:
                if loading:
                    for b in edge:
                        load(2, b).wait()
                        load(3, b).wait()
                head = basis[0].astype(F32) + above(k, 0)
                tail = basis[count - 1].astype(F32) + below(k, count - 1)
            fresh = [dot(inverse[b], side).astype(BF16) for b, side in zip(blocks, sides)]
            for b, value in zip(blocks, fresh):
                states[k, b + 1] = value
            if last:
                send_finals(blocks)
        if between is not None:
            between()

        @pl.when(has_left)
        def _():
            to_right(k - 1).wait_recv()

        @pl.when(has_right)
        def _():
            to_left(k - 1).wait_recv()

        head = (head + below(k, 0)).astype(BF16)
        tail = (tail + above(k, count - 1)).astype(BF16)
        head = dot(inverse[0], head).astype(BF16)
        tail = dot(inverse[count - 1], tail).astype(BF16)
        states[k, 1] = head
        states[k, count] = tail
        if last:
            send_finals(edge)
        else:
            send_halos(k)

    halves = [inner[: len(inner) // 2], inner[len(inner) // 2 :]]
    sweep(1, halves, loading=True)

    def middle(k, carry):
        sweep(k, [inner])
        return carry

    lax.fori_loop(2, SWEEPS - 1, middle, 0)

    def ends(blocks):
        sides = [(basis[b].astype(F32) + below(SWEEPS, b) + above(SWEEPS, b)).astype(BF16) for b in blocks]
        fresh = [dot(inverse[b], side).astype(BF16) for b, side in zip(blocks, sides)]
        for b, value in zip(blocks, fresh):
            states[SWEEPS, b + 1] = value
        send_finals(blocks)

    core = inner[2:-2]
    sweep(SWEEPS - 1, [inner], between=lambda: ends(core))
    rest = [b for b in inner if b not in core]
    outer = [b for b in rest if b in (inner[0], inner[-1])]
    sweep(SWEEPS, [outer, [b for b in rest if b not in outer]], last=True)

    def weighted(p, block):
        return block.astype(F32) * weights[p, 0:1, :]

    others = [lax.rem(pole + d, poles) for d in range(1, poles)]
    for p in others:
        send(
            weights.at[p], weights.at[p], weight_send.at[0], weight_recv.at[p], pole=p
        ).wait_recv()
    total = jnp.zeros((width, width), F32)
    for j in range(owned):
        block = weighted(pole, states[SWEEPS, pole * owned + j + 1])
        for p in others:
            send(
                got.at[p, j], got.at[p, j], final_send.at[0], final_recv.at[p, j], pole=p
            ).wait_recv()
            block = block + weighted(p, got[p, j])
        mine_ref[j * size : (j + 1) * size, :] = block
        total = total + lax.dot_general(
            block, block, (((0,), (0,)), ((), ())), precision=HIGHEST, preferred_element_type=F32
        )

    lines = width // poles
    for q in range(poles):
        partial[q] = total[q * lines : (q + 1) * lines, :]

    def share_to(d):
        q = lax.rem(pole + d, poles)
        return send(partial.at[q], shares.at[pole], share_send.at[d], share_recv.at[pole], pole=q)

    for d in range(1, poles):
        share_to(d).start()
    part = partial[pole]
    for p in others:
        send(shares.at[p], shares.at[p], share_send.at[0], share_recv.at[p], pole=p).wait_recv()
        part = part + shares[p]
    piece[...] = part

    def piece_to(d):
        q = lax.rem(row + d, rings)
        return send(piece, pieces.at[row], piece_send.at[d], piece_recv.at[row], row=q)

    for d in range(1, rings):
        piece_to(d).start()
    for d in range(1, rings):
        p = lax.rem(row + d, rings)
        send(pieces.at[p], pieces.at[p], piece_send.at[0], piece_recv.at[p], row=p).wait_recv()
        part = part + pieces[p]
    whole[pole] = part

    def whole_to(d):
        q = lax.rem(pole + d, poles)
        return send(whole.at[pole], whole.at[pole], whole_send.at[d], whole_recv.at[pole], pole=q)

    for d in range(1, poles):
        whole_to(d).start()
    for p in others:
        send(whole.at[p], whole.at[p], whole_send.at[0], whole_recv.at[p], pole=p).wait_recv()
    scale = 1.0 / (count * size * rings)
    for q in range(poles):
        gram_ref[q * lines : (q + 1) * lines, :] = whole[q] * scale

    for k in range(SWEEPS):

        @pl.when(has_left)
        def _():
            to_left(k).wait_send()

        @pl.when(has_right)
        def _():
            to_right(k).wait_send()

    for b in range(count):

        @pl.when(b // owned != pole)
        def _():
            final(b).wait_send()

    for d in range(1, poles):
        send(
            weights.at[pole], weights.at[pole], weight_send.at[d], weight_recv.at[pole], pole=lax.rem(pole + d, poles)
        ).wait_send()
        share_to(d).wait_send()
        whole_to(d).wait_send()
    for d in range(1, rings):
        piece_to(d).wait_send()


def sweeps_and_gram(basis, inverse, lower, upper, pole_weights):
    poles, rings = lax.axis_size("pole"), lax.axis_size("row")
    count, size, width = basis.shape
    owned = count // poles
    lines = width // poles
    dma = pltpu.SemaphoreType.DMA
    anywhere = pl.BlockSpec(memory_space=pl.ANY)
    return pl.pallas_call(
        functools.partial(sweep_kernel, poles, rings),
        out_shape=(
            jax.ShapeDtypeStruct((owned * size, width), F32),
            jax.ShapeDtypeStruct((width, width), F32),
        ),
        in_specs=[pl.BlockSpec(memory_space=pltpu.SMEM)] + [anywhere] * 4,
        out_specs=(pl.BlockSpec(memory_space=pltpu.VMEM),) * 2,
        scratch_shapes=[
            pltpu.VMEM((count, size, width), BF16),
            pltpu.VMEM((count, size, size), BF16),
            pltpu.VMEM((count, size, size), BF16),
            pltpu.VMEM((count, size, size), BF16),
            pltpu.VMEM((SWEEPS + 1, count + 2, size, width), BF16),
            pltpu.VMEM((poles, 8, width), F32),
            pltpu.VMEM((poles, owned, size, width), BF16),
            pltpu.VMEM((poles, lines, width), F32),
            pltpu.VMEM((poles, lines, width), F32),
            pltpu.VMEM((lines, width), F32),
            pltpu.VMEM((rings, lines, width), F32),
            pltpu.VMEM((poles, lines, width), F32),
            dma((4, count)),
            dma((SWEEPS, 2)),
            dma((SWEEPS, 2)),
            dma((poles,)),
            dma((poles,)),
            dma((count,)),
            dma((poles, owned)),
            dma((poles,)),
            dma((poles,)),
            dma((rings,)),
            dma((rings,)),
            dma((poles,)),
            dma((poles,)),
        ],
        compiler_params=pltpu.CompilerParams(collective_id=0, has_side_effects=True),
        name="sweeps",
    )(pole_weights, basis, inverse, lower, upper)


def inverse_factor(gram):
    n = gram.shape[0]
    lane = lax.broadcasted_iota(jnp.int32, (8, n), 1)
    sub = lax.broadcasted_iota(jnp.int32, (8, n), 0)
    lane1 = lane[0:1]
    rows = [gram[g:g+8] for g in range(0, n, 8)]
    for g in range(n // 8):
        base = 8 * g
        t = rows[g]
        cols = [jnp.broadcast_to(t[:, base+k:base+k+1], (8, n)) for k in range(8)]
        ratios, tops = {}, []
        for k in range(8):
            inv = 1.0 / cols[k][k:k+1]
            top = jnp.where(lane1 == base + k, inv, t[k:k+1] * inv)
            below = jnp.where(sub > k, cols[k], 0.0)
            t = jnp.where((lane == base + k) & (sub > k), 0.0, t) - below * top
            for l in range(k+1, 8):
                ratios[k, l] = cols[l][k:k+1] * inv
                cols[l] = cols[l] - below * ratios[k, l]
            tops.append(jnp.where((lane1 > base + k) & (lane1 < base + 8), 0.0, top))
        rows[g] = t
        inside = (lane >= base) & (lane < base + 8)
        for h in range(g+1, n // 8):
            t = rows[h]
            c = [jnp.broadcast_to(t[:, base+k:base+k+1], (8, n)) for k in range(8)]
            t = jnp.where(inside, 0.0, t)
            for k in range(8):
                t = t - c[k] * tops[k]
                for l in range(k+1, 8):
                    c[l] = c[l] - c[k] * ratios[k, l]
            rows[h] = t
    out = []
    for g, t in enumerate(rows):
        row = sub + 8 * g
        root = lax.rsqrt(jnp.sum(jnp.where(lane == row, t, 0.0), axis=1, keepdims=True))
        out.append(jnp.where(lane < row, t, jnp.where(lane == row, 1.0, 0.0)) * root)
    return jnp.concatenate(out, axis=0)


def solve_kernel(mine_ref, gram_ref, out_ref):
    inverse = inverse_factor(gram_ref[...])
    out_ref[...] = lax.dot_general(
        mine_ref[...], inverse, (((1,), (1,)), ((), ())), precision=HIGHEST, preferred_element_type=F32
    )


def orthonormalize(mine, gram):
    vmem = pl.BlockSpec(memory_space=pltpu.VMEM)
    return pl.pallas_call(
        solve_kernel,
        out_shape=jax.ShapeDtypeStruct(mine.shape, F32),
        in_specs=[vmem] * 2,
        out_specs=vmem,
        name="orthonormalize",
    )(mine, gram)


def shards(basis, inverses, lower, upper, pole_weights):
    rows, width = basis.shape
    count, size = inverses.shape[1], inverses.shape[-1]
    mine, gram = sweeps_and_gram(
        basis.reshape(count, size, width), inverses[0], lower, upper, pole_weights
    )
    return orthonormalize(mine, gram)


def solution(mesh):
    return jax.shard_map(
        shards,
        mesh=mesh,
        in_specs=(
            P("row", None),
            P("pole", "row", None, None),
            P("row", None, None),
            P("row", None, None),
            P("pole"),
        ),
        out_specs=P(("row", "pole"), None),
        check_vma=False,
    )
```
